256 devices in a mesh: azim: 16 (over z, y_hi), rad: 8 (over x, core), axial: 2 (over y_lo).
Axes of the slice: x: 4, y: 4 (y_hi: 2, y_lo: 2; y = y_hi * 2 + y_lo), z: 8, core: 2. Of those that a mesh axis runs over, the one named last changes fastest.
Arguments:
- residual: float32 [5, 512, 128, 256], P(None, 'azim', 'rad', 'axial'), may hold values from -12 to 12
- left_vec: float32 [5, 5], replicated, may hold values from -2.5 to 2.5
- dissip: float32 [5], replicated, may hold values from 0.2 to 0.5
- azim_coef: float32 [4, 5, 512], replicated, may hold values from 0 to 1, as said below
- radial_coef: float32 [2, 5, 128], replicated, may hold values from 0 to 3328
Outputs:
- update: float32 [5, 512, 128, 256], P(None, 'azim', 'rad', 'axial')
The draws below stay inside these ranges and needn't reach their ends.
Inputs may be any that keep to these rules, and one draw needn't show every extreme that they name: `azim_coef`: at every position a and b are positive with a + b < 1, and so are c and e with c + e < 1.
All inputs are finite; a program needn't handle non-finite values.
Results may differ from the reference program's by a relative error of at most 0.0003.
Values sent between devices are 32-bit elements; how exact they have to be, the bound alone decides.
A program may use at most 64 MiB of HBM per device.

```python
import math
import jax
import jax.numpy as jnp
from jax import lax

FIELD_COUNT = 5
CA = 32
CR = 16
AZIMUTH_CELLS = 512
NR = 128
NX = 256


def field_rates(key, fast_count):
    random_subkey_list = jax.random.split(key, 8)
    ranking = jax.random.permutation(random_subkey_list[0], FIELD_COUNT)
    fast_flag = (ranking < fast_count).astype(jnp.float32)[:, None]
    blocks = AZIMUTH_CELLS // CA
    slow_tau = AZIMUTH_CELLS * jnp.exp(jax.random.uniform(random_subkey_list[1], (FIELD_COUNT, 1), jnp.float32, math.log(2.0), math.log(4.0)))
    fast_tau = jnp.exp(jax.random.uniform(random_subkey_list[2], (FIELD_COUNT, 1), jnp.float32, math.log(8.0), math.log(16.0)))
    field_tau = fast_flag * fast_tau + (1.0 - fast_flag) * slow_tau
    block_factor = jnp.exp(jax.random.uniform(random_subkey_list[3], (FIELD_COUNT, blocks, 1), jnp.float32, math.log(0.7), math.log(1.4)))
    block_factor = jnp.broadcast_to(block_factor, (FIELD_COUNT, blocks, CA)).reshape(FIELD_COUNT, AZIMUTH_CELLS)
    cell_factor = jnp.exp(jax.random.uniform(random_subkey_list[4], (FIELD_COUNT, AZIMUTH_CELLS), jnp.float32, math.log(0.7), math.log(1.4)))
    tau_line = field_tau * block_factor * cell_factor
    retained = 1.0 - 1.0 / tau_line
    share_two = jax.random.uniform(random_subkey_list[5], (FIELD_COUNT, AZIMUTH_CELLS), jnp.float32, 0.1, 0.3)
    pulse_location = jax.random.randint(random_subkey_list[6], (FIELD_COUNT, 2), 0, AZIMUTH_CELLS)
    pulse_decay = jax.random.uniform(random_subkey_list[7], (FIELD_COUNT, 2), jnp.float32, 0.6, 0.8)
    cell_locations = jnp.arange(AZIMUTH_CELLS)
    impact_count = cell_locations[None, None, :] == pulse_location[:, :, None]
    damping_factor = jnp.prod(jnp.where(impact_count, pulse_decay[:, :, None], 1.0), axis=1)
    return (retained * (1.0 - share_two) * damping_factor, retained * share_two * damping_factor)


def draw_azim_coef(key, part):
    fast_count = jax.random.randint(jax.random.fold_in(key, 7), (), 1, 4)
    first, second = field_rates(jax.random.fold_in(key, 1), fast_count)
    third, fourth = field_rates(jax.random.fold_in(key, 2), fast_count)
    return jnp.stack([first, second, third, fourth])


def draw_radial_coef(key, part):
    random_subkey_list = jax.random.split(key, 6)
    fast_count = jax.random.randint(random_subkey_list[0], (), 1, 3)
    ranking = jax.random.permutation(random_subkey_list[1], FIELD_COUNT)
    fast_flag = (ranking < fast_count).astype(jnp.float32)[:, None]
    slow_len = CR * jnp.exp(jax.random.uniform(random_subkey_list[2], (FIELD_COUNT, 1), jnp.float32, math.log(1.5), math.log(2.5)))
    fast_len = jnp.exp(jax.random.uniform(random_subkey_list[3], (FIELD_COUNT, 1), jnp.float32, math.log(0.5), math.log(2.0)))
    length = fast_flag * fast_len + (1.0 - fast_flag) * slow_len
    strength = length * length
    lower = strength * jnp.exp(jax.random.uniform(random_subkey_list[4], (FIELD_COUNT, NR), jnp.float32, math.log(0.5), math.log(2.0)))
    upper = strength * jnp.exp(jax.random.uniform(random_subkey_list[5], (FIELD_COUNT, NR), jnp.float32, math.log(0.5), math.log(2.0)))
    return jnp.stack([lower, upper])


def draw_residual(key, part):
    random_subkey_list = jax.random.split(key, 1)
    noise = jax.random.normal(random_subkey_list[0], (FIELD_COUNT, AZIMUTH_CELLS, NR, NX), jnp.float32)
    values = noise
    return jnp.clip(values, -12.0, 12.0)


def centred(rng, extent, deviation, most, held_as=jnp.bfloat16):
    result = deviation * jax.random.normal(rng, extent, jnp.float32)
    return jnp.clip(result, min=-most, max=most).astype(held_as)


def setup_inputs(seed: int = 0) -> dict:
    splits = jax.random.split(jax.random.key(seed), 6)
    residual = draw_residual(jax.random.fold_in(splits[5], 71), 0)
    left_vec = centred(splits[1], (FIELD_COUNT, FIELD_COUNT), FIELD_COUNT ** -0.5, 2.5, jnp.float32)
    dissip = jnp.clip(jnp.exp(jax.random.uniform(splits[2], (FIELD_COUNT,), jnp.float32, math.log(0.2), math.log(0.5))), 0.2, 0.5)
    azim_coef = draw_azim_coef(jax.random.fold_in(splits[5], 71), 0)
    radial_coef = draw_radial_coef(jax.random.fold_in(splits[5], 71), 0)
    return {"residual": residual, "left_vec": left_vec, "dissip": dissip, "azim_coef": azim_coef, "radial_coef": radial_coef}


def azim_solve(source, first_coef, second_coef, direction):
    identity = jnp.eye(AZIMUTH_CELLS, dtype=jnp.float32)
    one_step = jnp.roll(identity, -direction, axis=1)
    two_step = jnp.roll(identity, -2 * direction, axis=1)
    matrix = identity[None] - first_coef[:, :, None] * one_step[None] - second_coef[:, :, None] * two_step[None]
    weights = jnp.sqrt(1.0 - (first_coef + second_coef) ** 2)
    right_side = (source * weights[:, :, None, None]).reshape(FIELD_COUNT, AZIMUTH_CELLS, NR * NX)
    solved = jnp.linalg.solve(matrix, right_side)
    return solved.reshape(FIELD_COUNT, AZIMUTH_CELLS, NR, NX)

def reference(residual, left_vec, dissip, azim_coef, radial_coef):
    characteristic = jnp.einsum('gf,farx->garx', left_vec, residual, precision=lax.Precision.HIGHEST)
    padded = jnp.pad(characteristic, ((0, 0), (0, 0), (0, 0), (1, 1)))
    source = characteristic + dissip[:, None, None, None] * (padded[..., 2:] + padded[..., :-2] - 2.0 * characteristic)
    lower_out = azim_solve(source, azim_coef[0], azim_coef[1], 1)
    upper_out = azim_solve(lower_out, azim_coef[2], azim_coef[3], -1)
    lower_rad = radial_coef[0]
    upper_rad = radial_coef[1]
    diagonal = 1.0 + lower_rad + upper_rad
    row_scale = diagonal ** 0.25
    below_diag = jnp.concatenate([jnp.zeros_like(lower_rad[:, :1]), -lower_rad[:, 1:]], axis=1)
    above_diag = jnp.concatenate([-upper_rad[:, :-1], jnp.zeros_like(upper_rad[:, :1])], axis=1)
    batch_shape = (FIELD_COUNT, AZIMUTH_CELLS, NR)
    return lax.linalg.tridiagonal_solve(jnp.broadcast_to(below_diag[:, None, :], batch_shape), jnp.broadcast_to(diagonal[:, None, :], batch_shape), jnp.broadcast_to(above_diag[:, None, :], batch_shape), upper_out * row_scale[:, None, :, None])
```

```python
import jax
import jax.numpy as jnp
from jax import lax
from jax.experimental import pallas as pl
from jax.experimental.pallas import tpu as pltpu
from jax.sharding import PartitionSpec as P

MESH = pl.DeviceIdType.MESH
F = 5
NA, NR, NX = 16, 8, 2
CA, CR, LX = 32, 16, 128
G = CA // NR
QA = 24
QR = 2 * F * G
f32 = jnp.float32


def lane_bcast(column, rows):
    return jnp.broadcast_to(column, (rows, LX))


def body(
    res_hbm, lv, dis, azc, rdc, out_hbm,
    x, obuf, xr, hs, hr, ct, cw, rt, rep, tab, traj, ktab, mt, rtraj, rtab, rmt,
    s1, r1, s2, r2, s3, r3, s4, r4,
    in_sem, out_sem, hsem, ss1, rs1, ss2, rs2, ss3, rs3, ss4, rs4,
):
    ia, ir, ix = lax.axis_index("azim"), lax.axis_index("rad"), lax.axis_index("axial")

    def azim_peer(d):
        return lax.rem(ia + d, NA)

    def rad_peer(d):
        return lax.rem(ir + d, NR)

    barrier = pltpu.get_barrier_semaphore()
    pl.semaphore_signal(barrier, inc=1, device_id={"axial": 1 - ix}, device_id_type=MESH)
    for d in range(1, NA):
        pl.semaphore_signal(barrier, inc=1, device_id={"azim": azim_peer(d)}, device_id_type=MESH)
    for d in range(1, NR):
        pl.semaphore_signal(barrier, inc=1, device_id={"rad": rad_peer(d)}, device_id_type=MESH)
    load = pltpu.make_async_copy(res_hbm, x, in_sem)
    load.start()

    pad = jnp.zeros((8 - F, NA * CA), f32)
    for c in range(4):
        ct[c] = jnp.transpose(jnp.concatenate([azc[c], pad], axis=0))
    cw[0] = jnp.sqrt(1.0 - (ct[0] + ct[1]) * (ct[0] + ct[1]))
    cw[1] = jnp.sqrt(1.0 - (ct[2] + ct[3]) * (ct[2] + ct[3]))
    mine = pl.ds(pl.multiple_of(ia * CA, CA), CA)
    for c in range(6):
        own = ct[c, mine] if c < 4 else cw[c - 4, mine]
        for f in range(F):
            tab[c, f] = lane_bcast(own[:, f : f + 1], CA)

    lane = lax.broadcasted_iota(jnp.int32, (CR, LX), 1)
    edge = (LX - 1) * (1 - ix)
    load.wait()

    def pack(i, held):
        first, second = held
        for k in range(4):
            a = i * 4 + k
            for f in range(F):
                place = 32 * (f % 4) + a
                turned = pltpu.roll(x[f, a], lax.rem(place + LX - edge, LX), 1)
                if f < 4:
                    first = jnp.where(lane == place, turned, first)
                else:
                    second = jnp.where(lane == place, turned, second)
        return first, second

    zero = jnp.zeros((CR, LX), f32)
    first, second = lax.fori_loop(0, CA // 4, pack, (zero, zero))
    hs[0:CR] = first
    hs[CR : 2 * CR] = second

    pl.semaphore_wait(barrier, NA + NR - 1)
    halo = pltpu.make_async_remote_copy(
        src_ref=hs, dst_ref=hr, send_sem=hsem.at[0], recv_sem=hsem.at[1],
        device_id={"axial": 1 - ix}, device_id_type=MESH,
    )
    halo.start()

    not_low = (lane != 0).astype(f32)
    not_high = (lane != LX - 1).astype(f32)

    def mix(i, _):
        for k in range(2):
            a = i * 2 + k
            old = [x[f, a] for f in range(F)]
            for g in range(F):
                c = lv[g, 0] * old[0]
                for f in range(1, F):
                    c = c + lv[g, f] * old[f]
                near = pltpu.roll(c, 1, 1) * not_low + pltpu.roll(c, LX - 1, 1) * not_high
                x[g, a] = c + dis[g] * (near - 2.0 * c)
        return 0

    lax.fori_loop(0, CA // 2, mix, 0)
    halo.wait()
    at_edge = (lane == edge).astype(f32)
    far = [pltpu.roll(hr[0:CR], (LX - 32 * f) % LX, 1) for f in range(4)] + [hr[CR : 2 * CR]]
    side = []
    for g in range(F):
        c = lv[g, 0] * far[0]
        for f in range(1, F):
            c = c + lv[g, f] * far[f]
        side.append(dis[g] * c)

    def row(ref, c, f, j):
        return jnp.broadcast_to(ref[c, f, pl.ds(j, 1), :], (CR, LX))

    def lower(i, state):
        one, two = list(state[:F]), list(state[F:])
        for k in range(4):
            j = i * 4 + k
            for f in range(F):
                here = x[f, j] + pltpu.roll(side[f], lax.rem(edge + LX - j, LX), 1) * at_edge
                now = row(tab, 4, f, j) * here + row(tab, 1, f, j) * two[f] + row(tab, 0, f, j) * one[f]
                x[f, j] = now
                one[f], two[f] = now, one[f]
        return tuple(one) + tuple(two)

    def upper(i, state):
        one, two = list(state[:F]), list(state[F:])
        for k in range(4):
            j = CA - 1 - (i * 4 + k)
            for f in range(F):
                now = row(tab, 5, f, j) * x[f, j] + row(tab, 3, f, j) * two[f] + row(tab, 2, f, j) * one[f]
                x[f, j] = now
                one[f], two[f] = now, one[f]
        return tuple(one) + tuple(two)

    nothing = (zero,) * (2 * F)
    low = lax.fori_loop(0, CA // 4, lower, nothing)
    high = lax.fori_loop(0, CA // 4, upper, nothing)
    leaving = list(low) + list(high)
    for v in range(4):
        for f in range(F):
            s1[pl.ds(v * F + f, NA, stride=QA), :] = leaving[v * F + f]
    for n in range(4 * F, QA):
        s1[pl.ds(n, NA, stride=QA), :] = zero

    def span(i, size):
        return pl.ds(pl.multiple_of(i * size, 8), size)

    def exchange(src, dst, ssem, rsem, axis, peer, me, size):
        return pltpu.make_async_remote_copy(
            src_ref=src.at[span(peer, size)], dst_ref=dst.at[span(me, size)],
            send_sem=ssem.at[peer], recv_sem=rsem.at[me],
            device_id={axis: peer}, device_id_type=MESH,
        )

    def send_all(src, dst, ssem, rsem, axis):
        n, me, size = (NA, ia, QA) if axis == "azim" else (NR, ir, QR)
        for d in range(1, n):
            exchange(src, dst, ssem, rsem, axis, lax.rem(me + d, n), me, size).start()
        dst[span(me, size)] = src[span(me, size)]

    def receive_all(src, dst, ssem, rsem, axis):
        n, me, size = (NA, ia, QA) if axis == "azim" else (NR, ir, QR)
        for d in range(1, n):
            peer = lax.rem(me + d, n)
            pltpu.make_async_remote_copy(
                src_ref=src.at[span(peer, size)], dst_ref=dst.at[span(peer, size)],
                send_sem=ssem.at[peer], recv_sem=rsem.at[peer],
                device_id={axis: peer}, device_id_type=MESH,
            ).wait()

    send_all(s1, r1, ss1, rs1, "azim")

    nil, unit = jnp.zeros((NA, 8), f32), jnp.ones((NA, 8), f32)

    def step_rows(ref, c, j):
        return ref[c, pl.ds(j, NA, stride=CA), :]

    first_low, second_low = [(unit, nil), (nil, unit)], []
    path = []
    for e in range(2):
        one, two = first_low[e]
        steps = []
        for j in range(CA):
            now = step_rows(ct, 0, j) * one + step_rows(ct, 1, j) * two
            steps.append(now)
            one, two = now, one
        path.append(steps)
    maps = [path[0][CA - 1], path[1][CA - 1], path[0][CA - 2], path[1][CA - 2]]
    cross, turn = [], []
    for e in range(4):
        one, two = [(nil, nil), (nil, nil), (unit, nil), (nil, unit)][e]
        for j in range(CA - 1, -1, -1):
            now = step_rows(ct, 2, j) * one + step_rows(ct, 3, j) * two
            if e < 2:
                now = now + step_rows(cw, 1, j) * path[e][j]
            traj[e, j * NA : (j + 1) * NA] = now
            one, two = now, one
        (cross if e < 2 else turn).append((one, two))
    maps += [cross[0][0], cross[1][0], cross[0][1], cross[1][1]]
    maps += [turn[0][0], turn[1][0], turn[0][1], turn[1][1]]
    maps = [jnp.transpose(m) for m in maps]
    M, X, N = maps[0:4], maps[4:8], maps[8:12]

    def column(m, k):
        return lane_bcast(m[:, k : k + 1], 8)

    def times(p, q):
        return [
            p[0] * q[0] + p[1] * q[2], p[0] * q[1] + p[1] * q[3],
            p[2] * q[0] + p[3] * q[2], p[2] * q[1] + p[3] * q[3],
        ]

    def closing(total):
        a, b, c, d = 1.0 - total[0], -total[1], -total[2], 1.0 - total[3]
        inverse = 1.0 / (a * d - b * c)
        return [d * inverse, -b * inverse, -c * inverse, a * inverse]

    for k in range(NA):
        for n in range(12):
            mt[n, k] = column(maps[n], k)
    ones, zeros = jnp.ones((8, LX), f32), jnp.zeros((8, LX), f32)
    run = [ones, zeros, zeros, ones]
    for k in range(NA):
        for n in range(4):
            mt[12 + n, k] = run[n]
        run = times([mt[n, k] for n in range(4)], run)
    close_low = closing(run)
    run = [ones, zeros, zeros, ones]
    for k in range(NA - 1, -1, -1):
        for n in range(4):
            mt[16 + n, k] = run[n]
        run = times([mt[8 + n, k] for n in range(4)], run)
    close_high = closing(run)
    for e in range(4):
        own = traj[e, pl.ds(ia, CA, stride=NA), :]
        for f in range(F):
            ktab[e, f] = lane_bcast(own[:, f : f + 1], CA)

    for c in range(2):
        for f in range(F):
            rep[c, f * G : (f + 1) * G] = jnp.broadcast_to(rdc[c, f : f + 1, :], (G, LX))
        rep[c, F * G :] = jnp.zeros((24 - F * G, LX), f32)
        rt[c] = jnp.transpose(rep[c])
    keep = jnp.ones((NR, 24), f32)
    lead = keep
    ys, cs = [], []
    for i in range(CR):
        l = rt[0, pl.ds(i, NR, stride=CR), :]
        u = rt[1, pl.ds(i, NR, stride=CR), :]
        s = 1.0 + l * keep
        r = 1.0 / (s + u)
        keep = s * r
        c = u * r
        la = l * r
        lead = la * lead
        ys.append(lead)
        cs.append(c)
        rtraj[0, i * NR : (i + 1) * NR] = jnp.sqrt(jnp.sqrt(1.0 + l + u)) * r
        rtraj[1, i * NR : (i + 1) * NR] = la
        rtraj[2, i * NR : (i + 1) * NR] = c
    left, right = jnp.zeros((NR, 24), f32), jnp.ones((NR, 24), f32)
    lefts, rights = [None] * CR, [None] * CR
    for i in range(CR - 1, -1, -1):
        left = ys[i] + cs[i] * left
        right = cs[i] * right
        lefts[i], rights[i] = left, right
        rtraj[3, i * NR : (i + 1) * NR] = left
        rtraj[4, i * NR : (i + 1) * NR] = right
    for e in range(5):
        own = rtraj[e, pl.ds(ir, CR, stride=NR), :]
        for f in range(F):
            rtab[e, f] = lane_bcast(own[:, f * G : f * G + 1], CR)
    ends = [jnp.transpose(m) for m in (lefts[0], rights[0], lefts[CR - 1], rights[CR - 1])]
    beta = jnp.zeros((24, LX), f32)
    for k in range(NR):
        l0, r0, l1, rr1 = [lane_bcast(m[:, k : k + 1], 24) for m in ends]
        gamma = 1.0 / (1.0 - l0 * beta)
        h = gamma * r0
        rmt[0, k], rmt[1, k], rmt[2, k], rmt[3, k] = l0, l1, gamma, h
        beta = rr1 + l1 * beta * h
        rmt[4, k] = beta

    receive_all(s1, r1, ss1, rs1, "azim")

    def part(k, v):
        return r1[pl.ds(k * QA + v * F, 8), :]

    def apply(m, k, one, two):
        return (mt[m, k] * one + mt[m + 1, k] * two, mt[m + 2, k] * one + mt[m + 3, k] * two)

    def through(m, one, two):
        return (m[0] * one + m[1] * two, m[2] * one + m[3] * two)

    one, two = zeros, zeros
    entering = []
    for k in range(NA):
        entering.append((one, two))
        p, q = apply(0, k, one, two)
        one, two = p + part(k, 0), q + part(k, 1)
    start = through(close_low, one, two)
    above = []
    for k in range(NA):
        p, q = apply(12, k, *start)
        p, q = entering[k][0] + p, entering[k][1] + q
        s2[pl.ds(k * QA, F), :] = p[0:F]
        s2[pl.ds(k * QA + F, F), :] = q[0:F]
        c, d = apply(4, k, p, q)
        above.append((c + part(k, 2), d + part(k, 3)))
    one, two = zeros, zeros
    for k in range(NA - 1, -1, -1):
        entering[k] = (one, two)
        p, q = apply(8, k, one, two)
        one, two = p + above[k][0], q + above[k][1]
    start = through(close_high, one, two)
    for k in range(NA):
        p, q = apply(16, k, *start)
        p, q = entering[k][0] + p, entering[k][1] + q
        s2[pl.ds(k * QA + 2 * F, F), :] = p[0:F]
        s2[pl.ds(k * QA + 3 * F, F), :] = q[0:F]
        s2[pl.ds(k * QA + 4 * F, QA - 4 * F), :] = zeros[0 : QA - 4 * F]

    send_all(s2, r2, ss2, rs2, "azim")
    receive_all(s2, r2, ss2, rs2, "azim")

    for f in range(F):
        enter = [r2[pl.ds(v * F + f, NA, stride=QA), :] for v in range(4)]

        def correct(i, _):
            for k in range(4):
                j = i * 4 + k
                at = pl.ds(pl.multiple_of((f * CA + j) * CR, CR), CR)
                total = x[f, j] + row(ktab, 0, f, j) * enter[0] + row(ktab, 1, f, j) * enter[1]
                xr[at, :] = total + row(ktab, 2, f, j) * enter[2] + row(ktab, 3, f, j) * enter[3]
            return 0

        lax.fori_loop(0, CA // 4, correct, 0)

    def rrow(e, f, i):
        return jnp.broadcast_to(rtab[e, f, pl.ds(i, 1), :], (8, LX))

    for f in range(F):
        ys = [[None] * CR for _ in range(G)]
        for g in range(G):
            y = None
            for i in range(CR):
                v = xr[pl.ds((f * CA + g * 8) * CR + i, 8, stride=CR), :] * rrow(0, f, i)
                y = v if y is None else v + rrow(1, f, i) * y
                ys[g][i] = y
            s3[pl.ds(F * G + f * G + g, NR, stride=QR), :] = y
            obuf[f, CR - 1, g * 8 : (g + 1) * 8] = y
            for i in range(CR - 2, -1, -1):
                y = ys[g][i] + rrow(2, f, i) * y
                obuf[f, i, g * 8 : (g + 1) * 8] = y
            s3[pl.ds(f * G + g, NR, stride=QR), :] = y

    send_all(s3, r3, ss3, rs3, "rad")
    receive_all(s3, r3, ss3, rs3, "rad")

    n = F * G
    alpha = jnp.zeros((n, LX), f32)
    gs, alphas = [], []
    for k in range(NR):
        first = r3[pl.ds(k * QR, n), :]
        last = r3[pl.ds(k * QR + n, n), :]
        g = rmt[2, k, 0:n] * (first + rmt[0, k, 0:n] * alpha)
        if k == 0:
            alpha = last
        else:
            alpha = last + rmt[1, k, 0:n] * (alpha + rmt[4, k - 1, 0:n] * g)
        gs.append(g)
        alphas.append(alpha)
    after = jnp.zeros((n, LX), f32)
    s4[pl.ds(0, n), :] = after
    for k in range(NR - 1, -1, -1):
        s4[pl.ds(k * QR + n, n), :] = after
        if k + 1 < NR:
            s4[pl.ds((k + 1) * QR, n), :] = alphas[k] + rmt[4, k, 0:n] * after
        after = gs[k] + rmt[3, k, 0:n] * after

    send_all(s4, r4, ss4, rs4, "rad")
    receive_all(s4, r4, ss4, rs4, "rad")

    stores = []
    for f in range(F):
        for g in range(G):
            before = r4[pl.ds(f * G + g, NR, stride=QR), :]
            behind = r4[pl.ds(n + f * G + g, NR, stride=QR), :]
            for i in range(CR):
                v = obuf[f, i, g * 8 : (g + 1) * 8] + rrow(3, f, i) * before + rrow(4, f, i) * behind
                xr[pl.ds((f * CA + g * 8) * CR + i, 8, stride=CR), :] = v
        rows = CA * CR
        store = pltpu.make_async_copy(xr.at[pl.ds(f * rows, rows)], out_hbm.at[pl.ds(f * rows, rows)], out_sem.at[f])
        store.start()
        stores.append(store)
    for store in stores:
        store.wait()


def local(residual, left_vec, dissip, azim_coef, radial_coef):
    vm = pltpu.VMEM
    dma = pltpu.SemaphoreType.DMA
    smem = pl.BlockSpec(memory_space=pltpu.SMEM)
    whole = pl.BlockSpec(memory_space=pltpu.VMEM)
    out = pl.pallas_call(
        body,
        out_shape=jax.ShapeDtypeStruct((F * CA * CR, LX), f32),
        in_specs=[pl.BlockSpec(memory_space=pl.ANY), smem, smem, whole, whole],
        out_specs=pl.BlockSpec(memory_space=pl.ANY),
        scratch_shapes=[
            vm((F, CA, CR, LX), f32),
            vm((F, CR, CA, LX), f32),
            vm((F * CA * CR, LX), f32),
            vm((2 * CR, LX), f32), vm((2 * CR, LX), f32),
            vm((4, NA * CA, 8), f32), vm((2, NA * CA, 8), f32),
            vm((2, NR * CR, 24), f32), vm((2, 24, NR * CR), f32),
            vm((6, F, CA, LX), f32),
            vm((4, CA * NA, 8), f32),
            vm((4, F, CA, LX), f32),
            vm((20, NA, 8, LX), f32),
            vm((5, CR * NR, 24), f32),
            vm((5, F, CR, LX), f32),
            vm((5, NR, 24, LX), f32),
            vm((NA * QA, LX), f32), vm((NA * QA, LX), f32),
            vm((NA * QA, LX), f32), vm((NA * QA, LX), f32),
            vm((NR * QR, LX), f32), vm((NR * QR, LX), f32),
            vm((NR * QR, LX), f32), vm((NR * QR, LX), f32),
            dma, dma((F,)), dma((2,)),
            dma((NA,)), dma((NA,)), dma((NA,)), dma((NA,)),
            dma((NR,)), dma((NR,)), dma((NR,)), dma((NR,)),
        ],
        compiler_params=pltpu.CompilerParams(
            collective_id=0, has_side_effects=True, vmem_limit_bytes=48 * 1024 * 1024
        ),
        name="adi",
    )(residual, left_vec, dissip, azim_coef, radial_coef)
    return out.reshape(F, CA, CR, LX)


def solution(mesh):
    placed = (P(None, "azim", "rad", "axial"), P(), P(), P(), P())
    return jax.shard_map(
        local,
        mesh=mesh,
        in_specs=placed,
        out_specs=P(None, "azim", "rad", "axial"),
        check_vma=False,
    )
```

```python
import jax
import jax.numpy as jnp
from jax import lax
from jax.experimental import pallas as pl
from jax.experimental.pallas import tpu as pltpu
from jax.sharding import PartitionSpec as P

MESH = pl.DeviceIdType.MESH
F = 5
NA, NR = 16, 8
CA, CR, LX = 32, 16, 128
G = CA // NR
NV = 4
QA = 24
QB = 2 * F * G
QE = 8
f32 = jnp.float32


def lane_bcast(column, rows):
    return jnp.broadcast_to(column, (rows, LX))


def body(
    res_hbm, lv_hbm, dis_hbm, azc_hbm, rdc_hbm, out,
    x, lvs, diss, azv, rdv, cat, own6, hs, hr, es, ee, ct, rt, rep, tab, traj, ktab, mt, rtraj, rtab, rline, rmt,
    s1, r1, s2, r2, sb1, rb1, sb2, rb2, s3, r3, s4, r4, eloc, re,
    in_sem, hsem, ss1, rs1, sse, rse, ss2, rs2, ssb1, rsb1, ssb2, rsb2, ss3, rs3, ss4, rs4,
):
    ia, ir, ix = lax.axis_index("azim"), lax.axis_index("rad"), lax.axis_index("axial")
    other = 1 - ix

    barrier = pltpu.get_barrier_semaphore()
    for d in range(NA - 1, -1, -1):
        peer = lax.rem(ia + d, NA)
        pl.semaphore_signal(barrier, inc=1, device_id={"azim": peer, "axial": other}, device_id_type=MESH)
        if d:
            pl.semaphore_signal(barrier, inc=1, device_id={"azim": peer}, device_id_type=MESH)
    for d in range(1, NR):
        pl.semaphore_signal(barrier, inc=1, device_id={"rad": lax.rem(ir + d, NR)}, device_id_type=MESH)
    loads = [
        pltpu.make_async_copy(src, dst, in_sem.at[n])
        for n, (src, dst) in enumerate(
            [(azc_hbm, azv), (lv_hbm, lvs), (dis_hbm, diss), (res_hbm, x), (rdc_hbm, rdv)]
        )
    ]
    for load in loads:
        load.start()
    lane = lax.broadcasted_iota(jnp.int32, (CR, LX), 1)
    edge = (LX - 1) * (1 - ix)
    not_low = (lane != 0).astype(f32)
    not_high = (lane != LX - 1).astype(f32)
    at_edge = (lane == edge).astype(f32)
    zero = jnp.zeros((CR, LX), f32)

    loads[0].wait()
    for c in range(4):
        for f in range(F):
            cat[c, f : f + 1, :] = azv[f, c : c + 1, :]
        cat[c, F:8, :] = jnp.zeros((8 - F, NA * CA), f32)
    group = pl.ds(pl.multiple_of((ia // 4) * LX, LX), LX)
    back = lax.rem(LX - lax.rem(ia, 4) * CA, LX)
    own = [pltpu.roll(cat[c, :, group], back, 1) for c in range(4)]
    own.append(jnp.sqrt(1.0 - (own[0] + own[1]) * (own[0] + own[1])))
    own.append(jnp.sqrt(1.0 - (own[2] + own[3]) * (own[2] + own[3])))
    for c in range(6):
        own6[c * 8 : (c + 1) * 8] = own[c]
    turned = jnp.transpose(own6[...])[0:CA]
    for c in range(6):
        for f in range(F):
            tab[c, f] = lane_bcast(turned[:, c * 8 + f : c * 8 + f + 1], CA)

    def row(ref, c, f, j):
        return jnp.broadcast_to(ref[c, f, pl.ds(j, 1), :], (CR, LX))

    for load in loads[1:4]:
        load.wait()
    lv = [[lvs[g, f] for f in range(F)] for g in range(F)]
    dis = [diss[f] for f in range(F)]

    def lower(i, state):
        one, two = list(state[:F]), list(state[F:])
        for k in range(4):
            j = i * 4 + k
            old = [x[f, j] for f in range(F)]
            for g in range(F):
                c = lv[g][0] * old[0]
                for f in range(1, F):
                    c = c + lv[g][f] * old[f]
                now = row(tab, 4, g, j) * c + row(tab, 1, g, j) * two[g] + row(tab, 0, g, j) * one[g]
                x[g, j] = now
                one[g], two[g] = now, one[g]
        return tuple(one) + tuple(two)

    def upper(i, state):
        one, two = list(state[:F]), list(state[F:])
        for k in range(4):
            j = CA - 1 - (i * 4 + k)
            for f in range(F):
                now = row(tab, 5, f, j) * x[f, j] + row(tab, 3, f, j) * two[f] + row(tab, 2, f, j) * one[f]
                x[f, j] = now
                one[f], two[f] = now, one[f]
        return tuple(one) + tuple(two)

    nothing = (zero,) * (2 * F)
    low = lax.fori_loop(0, CA // 4, lower, nothing)
    high = lax.fori_loop(0, CA // 4, upper, nothing)

    def damped(v, f):
        near = pltpu.roll(v, 1, 1) * not_low + pltpu.roll(v, LX - 1, 1) * not_high
        return v + dis[f] * (near - 2.0 * v)

    edges = zero
    for n, v in enumerate(list(low) + list(high)):
        edges = jnp.where(lane == n, pltpu.roll(v, lax.rem(n + LX - edge, LX), 1), edges)
        s1[pl.ds(n, NA, stride=QA), :] = damped(v, n % F)
    for n in range(NV * F, QA):
        s1[pl.ds(n, NA, stride=QA), :] = zero
    for o in range(NA):
        es[o] = edges[o : o + 1]

    def span(i, size):
        return pl.ds(pl.multiple_of(i * size, 8), size)

    def copies(src, dst, ssem, rsem, axis, size):
        n, me = (NA, ia) if axis == "azim" else (NR, ir)
        out_going, in_coming = [], []
        for d in range(1, n):
            peer = lax.rem(me + d, n)
            for place, into in ((me, out_going), (peer, in_coming)):
                into.append(
                    pltpu.make_async_remote_copy(
                        src_ref=src.at[span(peer, size)], dst_ref=dst.at[span(place, size)],
                        send_sem=ssem.at[peer], recv_sem=rsem.at[place],
                        device_id={axis: peer}, device_id_type=MESH,
                    )
                )

        def send():
            for copy in out_going:
                copy.start()
            dst[span(me, size)] = src[span(me, size)]

        def receive():
            for copy in in_coming:
                copy.wait_recv()

        def finish():
            for copy in out_going:
                copy.wait_send()

        return send, receive, finish

    edge_out, edge_in = [], []
    for d in range(NA):
        peer = lax.rem(ia + d, NA)
        for place, into in ((ia, edge_out), (peer, edge_in)):
            into.append(
                pltpu.make_async_remote_copy(
                    src_ref=es.at[peer], dst_ref=ee.at[place], send_sem=sse.at[peer], recv_sem=rse.at[place],
                    device_id={"azim": peer, "axial": other}, device_id_type=MESH,
                )
            )
    send1, receive1, finish1 = copies(s1, r1, ss1, rs1, "azim", QA)
    send2, receive2, finish2 = copies(s2, r2, ss2, rs2, "azim", QA)
    sendb1, receiveb1, finishb1 = copies(sb1, rb1, ssb1, rsb1, "rad", QB)
    sendb2, receiveb2, finishb2 = copies(sb2, rb2, ssb2, rsb2, "rad", QB)
    send3, receive3, finish3 = copies(s3, r3, ss3, rs3, "rad", QE)
    send4, receive4, finish4 = copies(s4, r4, ss4, rs4, "rad", QE)

    pl.semaphore_wait(barrier, 2 * NA + NR - 2)
    for copy in edge_out:
        copy.start()
    send1()

    def pack(i, held):
        first, second = held
        for k in range(4):
            a = i * 4 + k
            for f in range(F):
                place = 32 * (f % 4) + a
                moved = pltpu.roll(x[f, a], lax.rem(place + LX - edge, LX), 1)
                if f < 4:
                    first = jnp.where(lane == place, moved, first)
                else:
                    second = jnp.where(lane == place, moved, second)
        return first, second

    first, second = lax.fori_loop(0, CA // 4, pack, (zero, zero))
    hs[0:CR] = first
    hs[CR : 2 * CR] = second
    halo = pltpu.make_async_remote_copy(
        src_ref=hs, dst_ref=hr, send_sem=hsem.at[0], recv_sem=hsem.at[1],
        device_id={"axial": other}, device_id_type=MESH,
    )
    halo.start()

    for c in range(4):
        ct[c] = jnp.transpose(cat[c])
    nil, unit = jnp.zeros((NA, 8), f32), jnp.ones((NA, 8), f32)

    def step_rows(c, j):
        return ct[c, pl.ds(j, NA, stride=CA), :]

    path = []
    for one, two in ((unit, nil), (nil, unit)):
        steps = []
        for j in range(CA):
            now = step_rows(0, j) * one + step_rows(1, j) * two
            steps.append(now)
            one, two = now, one
        path.append(steps)
    maps = [path[0][CA - 1], path[1][CA - 1], path[0][CA - 2], path[1][CA - 2]]
    state = [(nil, nil), (nil, nil), (unit, nil), (nil, unit)]
    for j in range(CA - 1, -1, -1):
        c, e = step_rows(2, j), step_rows(3, j)
        w = jnp.sqrt(1.0 - (c + e) * (c + e))
        for n in range(4):
            one, two = state[n]
            now = c * one + e * two
            if n < 2:
                now = now + w * path[n][j]
            traj[n, j * NA : (j + 1) * NA] = now
            state[n] = (now, one)
    maps += [state[0][0], state[1][0], state[0][1], state[1][1]]
    maps += [state[2][0], state[3][0], state[2][1], state[3][1]]
    maps = [jnp.transpose(m) for m in maps]

    def column(m, k):
        return lane_bcast(m[:, k : k + 1], 8)

    def times(p, q):
        return [
            p[0] * q[0] + p[1] * q[2], p[0] * q[1] + p[1] * q[3],
            p[2] * q[0] + p[3] * q[2], p[2] * q[1] + p[3] * q[3],
        ]

    def closing(total):
        a, b, c, d = 1.0 - total[0], -total[1], -total[2], 1.0 - total[3]
        inverse = 1.0 / (a * d - b * c)
        return [d * inverse, -b * inverse, -c * inverse, a * inverse]

    for k in range(NA):
        for n in range(12):
            mt[n, k] = column(maps[n], k)
    ones, zeros = jnp.ones((8, LX), f32), jnp.zeros((8, LX), f32)
    run = [ones, zeros, zeros, ones]
    for k in range(NA):
        for n in range(4):
            mt[12 + n, k] = run[n]
        run = times([mt[n, k] for n in range(4)], run)
    close_low = closing(run)
    run = [ones, zeros, zeros, ones]
    for k in range(NA - 1, -1, -1):
        for n in range(4):
            mt[16 + n, k] = run[n]
        run = times([mt[8 + n, k] for n in range(4)], run)
    close_high = closing(run)
    for e in range(NV):
        own = traj[e, pl.ds(ia, CA, stride=NA), :]
        for f in range(F):
            ktab[e, f] = lane_bcast(own[:, f : f + 1], CA)

    loads[4].wait()
    for c in range(2):
        for n in range(QA):
            rep[c, n : n + 1, :] = rdv[n % F, c : c + 1, :]
        rt[c] = jnp.transpose(rep[c])
    keep = jnp.ones((NR, QA), f32)
    lead = keep
    ys, cs = [], []
    for i in range(CR):
        l = rt[0, pl.ds(i, NR, stride=CR), :]
        u = rt[1, pl.ds(i, NR, stride=CR), :]
        s = 1.0 + l * keep
        r = 1.0 / (s + u)
        keep = s * r
        c = u * r
        la = l * r
        lead = la * lead
        ys.append(lead)
        cs.append(c)
        rtraj[0, i * NR : (i + 1) * NR] = jnp.sqrt(jnp.sqrt(1.0 + l + u)) * r
        rtraj[1, i * NR : (i + 1) * NR] = la
        rtraj[2, i * NR : (i + 1) * NR] = c
    left, right = jnp.zeros((NR, QA), f32), jnp.ones((NR, QA), f32)
    lefts, rights = [None] * CR, [None] * CR
    for i in range(CR - 1, -1, -1):
        left = ys[i] + cs[i] * left
        right = cs[i] * right
        lefts[i], rights[i] = left, right
        rtraj[3, i * NR : (i + 1) * NR] = left
        rtraj[4, i * NR : (i + 1) * NR] = right
    for e in range(5):
        own = rtraj[e, pl.ds(ir, CR, stride=NR), :]
        for f in range(F):
            rtab[e, f] = lane_bcast(own[:, f : f + 1], CR)
        own = jnp.transpose(own)
        for i in range(CR):
            rline[e, i] = lane_bcast(own[:, i : i + 1], QA)
    ends = [jnp.transpose(m) for m in (lefts[0], rights[0], lefts[CR - 1], rights[CR - 1])]
    beta = jnp.zeros((QA, LX), f32)
    for k in range(NR):
        l0, r0, l1, rr1 = [lane_bcast(m[:, k : k + 1], QA) for m in ends]
        gamma = 1.0 / (1.0 - l0 * beta)
        h = gamma * r0
        beta = rr1 + l1 * beta * h
        for n, m in enumerate((l0, l1, gamma, h, beta)):
            rmt[n, k * QA : (k + 1) * QA] = m

    halo.wait_recv()
    far = [pltpu.roll(hr[0:CR], (LX - 32 * f) % LX, 1) for f in range(4)] + [hr[CR : 2 * CR]]
    side = [dis[f] * far[f] for f in range(F)]

    def dissipate(i, _):
        for k in range(2):
            a = i * 2 + k
            for f in range(F):
                x[f, a] = damped(x[f, a], f) + pltpu.roll(side[f], lax.rem(edge + LX - a, LX), 1) * at_edge
        return 0

    lax.fori_loop(0, CA // 2, dissipate, 0)

    line = lax.broadcasted_iota(jnp.int32, (QA, LX), 0)
    weight = jnp.zeros((QA, LX), f32)
    for n in range(NV * F):
        weight = jnp.where(line == n, dis[n % F], weight)
    weight = jnp.where(lax.broadcasted_iota(jnp.int32, (QA, LX), 1) == edge, weight, 0.0)

    for copy in edge_in:
        copy.wait_recv()
    receive1()
    beyond = jnp.transpose(ee[:, 0, :])[0:QA]
    for k in range(NA):
        at = pl.ds(k * QA, QA)
        r1[at, :] = r1[at, :] + lane_bcast(beyond[:, k : k + 1], QA) * weight

    def part(k, v):
        return r1[pl.ds(k * QA + v * F, 8), :]

    def apply(m, k, one, two):
        return (mt[m, k] * one + mt[m + 1, k] * two, mt[m + 2, k] * one + mt[m + 3, k] * two)

    def through(m, one, two):
        return (m[0] * one + m[1] * two, m[2] * one + m[3] * two)

    one, two = zeros, zeros
    entering = []
    for k in range(NA):
        entering.append((one, two))
        p, q = apply(0, k, one, two)
        one, two = p + part(k, 0), q + part(k, 1)
    start = through(close_low, one, two)
    above = []
    for k in range(NA):
        p, q = apply(12, k, *start)
        p, q = entering[k][0] + p, entering[k][1] + q
        s2[pl.ds(k * QA, F), :] = p[0:F]
        s2[pl.ds(k * QA + F, F), :] = q[0:F]
        c, d = apply(4, k, p, q)
        above.append((c + part(k, 2), d + part(k, 3)))
    one, two = zeros, zeros
    for k in range(NA - 1, -1, -1):
        entering[k] = (one, two)
        p, q = apply(8, k, one, two)
        one, two = p + above[k][0], q + above[k][1]
    start = through(close_high, one, two)
    for k in range(NA):
        p, q = apply(16, k, *start)
        p, q = entering[k][0] + p, entering[k][1] + q
        s2[pl.ds(k * QA + 2 * F, F), :] = p[0:F]
        s2[pl.ds(k * QA + 3 * F, F), :] = q[0:F]
        s2[pl.ds(k * QA + 4 * F, QA - 4 * F), :] = zeros[0 : QA - 4 * F]

    send2()

    def rrow(e, f, i, rows):
        return jnp.broadcast_to(rtab[e, f, pl.ds(i, 1), :], (rows, LX))

    flat = x.reshape(F * CA * CR, LX)
    for f in range(F):
        for g in range(G):
            def cells(i):
                return pl.ds((f * CA + g * 8) * CR + i, 8, stride=CR)

            ys, y = [], None
            for i in range(CR):
                v = flat[cells(i), :] * rrow(0, f, i, 8)
                y = v if y is None else v + rrow(1, f, i, 8) * y
                ys.append(y)
            sb1[pl.ds(F * G + g * F + f, NR, stride=QB), :] = y
            flat[cells(CR - 1), :] = y
            for i in range(CR - 2, -1, -1):
                y = ys[i] + rrow(2, f, i, 8) * y
                flat[cells(i), :] = y
            sb1[pl.ds(g * F + f, NR, stride=QB), :] = y
    sendb1()
    for n in (3, 7):
        s3[pl.ds(n, NR, stride=QE), :] = jnp.zeros((NR, LX), f32)
        s4[pl.ds(n, NR, stride=QE), :] = jnp.zeros((NR, LX), f32)

    def close_radial(src, dst, size, n, place, at):
        alpha = jnp.zeros((n, LX), f32)
        gs, alphas = [], []
        for k in range(NR):
            first = src[pl.ds(k * size, n), :]
            last = src[pl.ds(k * size + place, n), :]
            g = rmt[2, at(k), :] * (first + rmt[0, at(k), :] * alpha)
            if k == 0:
                alpha = last
            else:
                alpha = last + rmt[1, at(k), :] * (alpha + rmt[4, at(k - 1), :] * g)
            gs.append(g)
            alphas.append(alpha)
        after = jnp.zeros((n, LX), f32)
        dst[pl.ds(0, n), :] = after
        for k in range(NR - 1, -1, -1):
            dst[pl.ds(k * size + place, n), :] = after
            if k + 1 < NR:
                dst[pl.ds((k + 1) * size, n), :] = alphas[k] + rmt[4, at(k), :] * after
            after = gs[k] + rmt[3, at(k), :] * after

    receiveb1()
    close_radial(rb1, sb2, QB, F * G, F * G, lambda k: pl.ds(k * QA, F * G))
    sendb2()

    receive2()
    ys, y = [], None
    for i in range(CR):
        v = r2[pl.ds(i * QA, QA), :] * rline[0, i]
        y = v if y is None else v + rline[1, i] * y
        ys.append(y)
    eloc[CR - 1] = y
    for s in range(3):
        s3[pl.ds(4 + s, NR, stride=QE), :] = y[8 * s : 8 * s + 8]
    for i in range(CR - 2, -1, -1):
        y = ys[i] + rline[2, i] * y
        eloc[i] = y
    for s in range(3):
        s3[pl.ds(s, NR, stride=QE), :] = y[8 * s : 8 * s + 8]
    send3()
    receive3()
    close_radial(r3, s4, QE, 3, 4, lambda k: pl.ds(k * QA + ir, 3, stride=8))
    send4()

    receiveb2()
    for f in range(F):
        lefts = [rtab[3, f], rtab[4, f]]
        for a in range(CA):
            g, o = a // 8, a % 8
            sides = [
                jnp.broadcast_to(rb2[pl.ds(o * QB + v * F * G + g * F + f, 1), :], (CR, LX)) for v in range(2)
            ]
            x[f, a] = x[f, a] + lefts[0] * sides[0] + lefts[1] * sides[1]

    receive4()
    before = jnp.concatenate([r4[pl.ds(s, NR, stride=QE), :] for s in range(3)], axis=0)
    behind = jnp.concatenate([r4[pl.ds(4 + s, NR, stride=QE), :] for s in range(3)], axis=0)
    for i in range(CR):
        re[pl.ds(i * QA, QA), :] = eloc[i] + rline[3, i] * before + rline[4, i] * behind
    for f in range(F):
        enter = [re[pl.ds(v * F + f, CR, stride=QA), :] for v in range(NV)]
        for a in range(CA):
            total = x[f, a] + row(ktab, 0, f, a) * enter[0] + row(ktab, 1, f, a) * enter[1]
            out[f, a] = total + row(ktab, 2, f, a) * enter[2] + row(ktab, 3, f, a) * enter[3]

    for copy in edge_out:
        copy.wait_send()
    halo.wait_send()
    for finish in (finish1, finish2, finishb1, finishb2, finish3, finish4):
        finish()


def local(residual, left_vec, dissip, azim_coef, radial_coef):
    vm = pltpu.VMEM
    dma = pltpu.SemaphoreType.DMA
    hbm = pl.BlockSpec(memory_space=pltpu.HBM)
    return pl.pallas_call(
        body,
        out_shape=jax.ShapeDtypeStruct((F, CA, CR, LX), f32),
        in_specs=[hbm] * 5,
        out_specs=pl.BlockSpec(memory_space=pltpu.VMEM),
        scratch_shapes=[
            vm((F, CA, CR, LX), f32),
            pltpu.SMEM((F, F), f32), pltpu.SMEM((F,), f32),
            vm((F, 4, NA * CA), f32), vm((F, 2, NR * CR), f32),
            vm((4, 8, NA * CA), f32), vm((48, LX), f32),
            vm((2 * CR, LX), f32), vm((2 * CR, LX), f32),
            vm((NA, 1, LX), f32), vm((NA, 1, LX), f32),
            vm((4, NA * CA, 8), f32),
            vm((2, NR * CR, QA), f32), vm((2, QA, NR * CR), f32),
            vm((6, F, CA, LX), f32),
            vm((NV, CA * NA, 8), f32),
            vm((NV, F, CA, LX), f32),
            vm((20, NA, 8, LX), f32),
            vm((5, CR * NR, QA), f32),
            vm((5, F, CR, LX), f32),
            vm((5, CR, QA, LX), f32),
            vm((5, NR * QA, LX), f32),
            *[vm((NA * QA, LX), f32)] * 4,
            *[vm((NR * QB, LX), f32)] * 4,
            *[vm((NR * QE, LX), f32)] * 4,
            vm((CR, QA, LX), f32), vm((CR * QA, LX), f32),
            dma((5,)), dma((2,)),
            *[dma((NA,))] * 6,
            *[dma((NR,))] * 8,
        ],
        compiler_params=pltpu.CompilerParams(
            collective_id=0, has_side_effects=True, vmem_limit_bytes=63438848
        ),
        name="adi",
    )(
        residual, left_vec, dissip,
        jnp.transpose(azim_coef, (1, 0, 2)), jnp.transpose(radial_coef, (1, 0, 2)),
    )


def solution(mesh):
    placed = (P(None, "azim", "rad", "axial"), P(), P(), P(), P())
    return jax.shard_map(
        local,
        mesh=mesh,
        in_specs=placed,
        out_specs=P(None, "azim", "rad", "axial"),
        check_vma=False,
    )
```
